32 devices in a mesh: dp: 4 (over x, core), ctx: 4 (over z), tensor: 2 (over y).
Axes of the slice: x: 2, y: 2, z: 4, core: 2. Of those that a mesh axis runs over, the one named last changes fastest.
Arguments:
- query: bfloat16 [4, 512, 32, 128], P('dp', 'ctx', 'tensor'), may hold values from -200 to 200
- key_value: bfloat16 [2, 4, 512, 2, 128], P(None, 'dp', 'ctx'), may hold values from -7 to 7
- grad_out: bfloat16 [4, 512, 32, 128], P('dp', 'ctx', 'tensor'), may hold values from -6 to 6
- doc_lengths: int32 [4, 16], P('dp'), may hold values from 1 to 80, 512 in all within a row
- stretch_order: int32 [4, 4], P('dp'), may hold values from 0 to 3, each once within a row
- loss_mask: int32 [4, 512], P('dp', 'ctx'), may hold values from 0 to 1
Outputs:
- attended: bfloat16 [4, 512, 32, 128], P('dp', 'ctx', 'tensor')
- grad_query: bfloat16 [4, 512, 32, 128], P('dp', 'ctx', 'tensor')
- grad_key_value: bfloat16 [2, 4, 512, 2, 128], P(None, 'dp', 'ctx')
The draws below stay inside these ranges and needn't reach their ends.
Inputs may be any that keep to these rules, and one draw needn't show every extreme that they name: `doc_lengths`: each row sums to 512 and its largest entry is 80. `stretch_order`: each row names every block index of its sequence once.
All inputs are finite; a program needn't handle non-finite values.
Results may differ from the reference program's by a relative error of at most 0.03.
Values may be sent and summed in bfloat16 or wider, within the bound.
A program may use at most 64 MiB of HBM per device.

```python
import math
import jax
import jax.numpy as jnp
import numpy as np
from jax import lax

HEAD_DIM = 128
DOCS = 16
BATCH = 4
LENGTH = 512
HEADS = 32
KV_HEADS = 2
MOST = 80
N_CTX = 4


def shared_keys(base_key):
    folded = jax.random.fold_in(base_key, 11)
    key_rows = jnp.clip(jax.random.normal(jax.random.fold_in(folded, 1), (BATCH, LENGTH, KV_HEADS, HEAD_DIM), jnp.float32), -6.0, 6.0)
    return key_rows


def draw_key_value(key, part):
    key_rows = shared_keys(key)
    values = jnp.clip(jax.random.normal(jax.random.fold_in(key, 41), (BATCH, LENGTH, KV_HEADS, HEAD_DIM), jnp.float32), -6.0, 6.0)
    return jnp.stack([key_rows, values]).astype(jnp.bfloat16)


def draw_query(key, part):
    queries = jnp.clip(jax.random.normal(jax.random.fold_in(key, 21), (BATCH, LENGTH, HEADS, HEAD_DIM), jnp.float32), -6.0, 6.0)
    return queries.astype(jnp.bfloat16)


def draw_loss_mask(key, part):
    total = BATCH * LENGTH
    flat = jnp.arange(total, dtype=jnp.int32)
    level = jax.random.randint(jax.random.fold_in(key, 62), (), 100, 1001)
    member_level = jax.random.randint(jax.random.fold_in(key, 63), (BATCH,), 75, 101)
    member_of = flat // LENGTH
    member_factor = jnp.sum(jnp.where(member_of[:, None] == jnp.arange(BATCH, dtype=jnp.int32)[None, :], member_level[None, :], 0), axis=1)
    profile = 200 + 700 * flat // total
    threshold = level * member_factor * profile // 100000
    rolled = jax.random.randint(jax.random.fold_in(key, 61), (total,), 0, 1000)
    return (rolled < threshold).astype(jnp.int32).reshape(BATCH, LENGTH)


def steps_of(own_key, dims, shards, low, high):
    level = 1.0
    for position, shards_of in shards:
        draws = jax.random.uniform(jax.random.fold_in(jax.random.fold_in(own_key, 6), position), (shards_of,), jnp.float32, low / len(shards), high / len(shards))
        level = level * jnp.repeat(jnp.exp(draws), dims[position] // shards_of).reshape((-1,) + (1,) * (len(dims) - 1 - position))
    return level


def length_profile(count, total, reach, slope):
    weights = [(1 << 20) // math.isqrt(grade ** slope) + 1 for grade in range(2, count + 1)]
    spare, given = total - reach - (count - 1), [1] * (count - 1)
    while spare > 0:
        movable = [i for i in range(count - 1) if given[i] < reach]
        pool, remaining = sum([weights[i] for i in movable]), spare
        for i in movable:
            more = min(reach - given[i], max(1, remaining * weights[i] // pool), spare)
            given[i] = given[i] + more
            spare = spare - more
    return np.array([reach] + given)


def ragged(key, count, total, most, slope):
    if count == 2:
        one = jax.random.randint(key, (), max(1, total - most), min(most, total - 1) + 1)
        return jnp.stack([one, total - one])
    tallies = jnp.asarray(length_profile(count, total, most, slope), jnp.int32)
    couples = (count - 1) // 2
    giver, taker = tallies[1:1 + 2 * couples:2], tallies[2:2 + 2 * couples:2]
    slack = jnp.minimum(giver - 1, most - taker)
    shifted = jax.random.randint(jax.random.fold_in(key, 1), (couples,), 0, 1 << 20) % (slack + 1)
    tallies = tallies.at[1:1 + 2 * couples:2].set(giver - shifted).at[2:2 + 2 * couples:2].set(taker + shifted)
    return tallies[jax.random.permutation(jax.random.fold_in(key, 2), count)]


def noise(rng, shape, scale, reach, shards=(), kind=jnp.bfloat16):
    array = scale * jax.random.normal(rng, shape, jnp.float32)
    if shards:
        array = array * steps_of(rng, shape, shards, -0.22, 0.18)
    return jnp.clip(array, -reach, reach).astype(kind)


def setup_inputs(seed: int = 0) -> dict:
    key_of = jax.random.split(jax.random.key(seed), 7)
    query = draw_query(jax.random.fold_in(key_of[6], 71), 0)
    key_value = draw_key_value(jax.random.fold_in(key_of[6], 71), 0)
    grad_out = noise(key_of[2], (BATCH, LENGTH, HEADS, HEAD_DIM), 1.0, 6.0, ((0, 4), (1, 4), (2, 2)))
    doc_lengths = jax.vmap(lambda own: ragged(own, DOCS, LENGTH, MOST, 2))(jax.random.split(key_of[3], BATCH)).reshape((BATCH, DOCS)).astype(jnp.int32)
    stretch_order = jax.vmap(lambda own: jax.random.permutation(own, N_CTX))(jax.random.split(key_of[4], BATCH)).reshape((BATCH, N_CTX)).astype(jnp.int32)
    loss_mask = draw_loss_mask(jax.random.fold_in(key_of[6], 71), 0)
    return dict(query=query, key_value=key_value, grad_out=grad_out, doc_lengths=doc_lengths, stretch_order=stretch_order, loss_mask=loss_mask)


def batched(left_side, right_side, pattern):
    return jnp.einsum(pattern, left_side.astype(jnp.float32), right_side.astype(jnp.float32), precision=lax.Precision.HIGHEST)

def reference(query, key_value, grad_out, doc_lengths, stretch_order, loss_mask):
    seq_count = query.shape[0]
    length = query.shape[1]
    head_count = query.shape[2]
    head_width = query.shape[3]
    kv_count = key_value.shape[3]
    group_size = head_count // kv_count
    shard_rows = length // N_CTX
    window = (MOST - 1 + shard_rows - 1) // shard_rows
    margin = window * shard_rows
    span_rows = margin + shard_rows
    factor = 1.0 / math.sqrt(head_width)
    counted = jnp.maximum(jnp.sum(loss_mask.astype(jnp.float32)), 1.0)
    weight = seq_count * length / counted
    ordinal = jnp.arange(length, dtype=jnp.int32)
    window_rows = jnp.arange(N_CTX, dtype=jnp.int32)[:, None] * shard_rows + jnp.arange(span_rows, dtype=jnp.int32)[None, :]
    key_places = window_rows - margin
    query_places = ordinal.reshape(N_CTX, shard_rows)
    flat_rows = window_rows.reshape(-1)
    attended_list = []
    query_list = []
    key_list = []
    value_list = []
    for member in range(seq_count):
        order_row = stretch_order[member]
        places = order_row[ordinal // shard_rows] * shard_rows + ordinal % shard_rows
        holder = jnp.zeros((N_CTX,), jnp.int32).at[order_row].set(jnp.arange(N_CTX, dtype=jnp.int32))
        sources = holder[ordinal // shard_rows] * shard_rows + ordinal % shard_rows
        bounds = jnp.cumsum(doc_lengths[member])
        doc_ids = lax.optimization_barrier(jnp.sum((bounds[None, :] <= ordinal[:, None]).astype(jnp.int32), axis=1))
        padded_docs = jnp.concatenate([jnp.full((margin,), -1, jnp.int32), doc_ids])
        visible = (doc_ids.reshape(N_CTX, shard_rows)[:, :, None] == padded_docs[window_rows][:, None, :]) & (key_places[:, None, :] <= query_places[:, :, None])
        scaled = (grad_out[member].astype(jnp.float32) * loss_mask[member][:, None, None].astype(jnp.float32) * weight).astype(jnp.bfloat16)
        queries_all = query[member][sources]
        upstream_all = scaled[sources]
        padding = jnp.zeros((2, margin, kv_count, head_width), key_value.dtype)
        pair_padded = jnp.concatenate([padding, key_value[:, member][:, sources]], axis=1)
        pair_window = pair_padded[:, window_rows]

        def per_head(head_index):
            queries = lax.dynamic_index_in_dim(queries_all, head_index, 1, keepdims=False).reshape(N_CTX, shard_rows, head_width)
            upstream = lax.dynamic_index_in_dim(upstream_all, head_index, 1, keepdims=False).reshape(N_CTX, shard_rows, head_width)
            group_index = head_index // group_size
            key_rows = lax.dynamic_index_in_dim(pair_window[0], group_index, 2, keepdims=False)
            values = lax.dynamic_index_in_dim(pair_window[1], group_index, 2, keepdims=False)
            scores = batched(queries, key_rows, 'cqd,ckd->cqk') * factor
            scores = jnp.where(visible, scores, -1e+30)
            highest = lax.optimization_barrier(jnp.max(scores, axis=2, keepdims=True))
            exponent = jnp.where(visible, jnp.exp(scores - highest), 0.0)
            probabilities = exponent / lax.optimization_barrier(jnp.sum(exponent, axis=2, keepdims=True))
            probs_low = probabilities.astype(jnp.bfloat16)
            output = batched(probs_low, values, 'cqk,ckd->cqd').astype(jnp.bfloat16)
            row_delta = lax.optimization_barrier(jnp.sum(upstream.astype(jnp.float32) * output.astype(jnp.float32), axis=2, keepdims=True))
            prob_grad = batched(upstream, values, 'cqd,ckd->cqk')
            score_grad = (probabilities * (prob_grad - row_delta)).astype(jnp.bfloat16)
            query_grad = (batched(score_grad, key_rows, 'cqk,ckd->cqd') * factor).astype(jnp.bfloat16)
            key_part = batched(score_grad, queries, 'cqk,cqd->ckd') * factor
            value_part = batched(probs_low, upstream, 'cqk,cqd->ckd')
            empty = jnp.zeros((margin + length, head_width), jnp.float32)
            key_grad = empty.at[flat_rows].add(key_part.reshape(-1, head_width))[margin:]
            value_grad = empty.at[flat_rows].add(value_part.reshape(-1, head_width))[margin:]
            return (output.reshape(length, head_width), query_grad.reshape(length, head_width), key_grad, value_grad)
        outputs, query_grads, key_grads, value_grads = lax.map(per_head, jnp.arange(head_count, dtype=jnp.int32))
        attended_list.append(jnp.transpose(outputs[:, places], (1, 0, 2)))
        query_list.append(jnp.transpose(query_grads[:, places], (1, 0, 2)))
        key_sum = lax.optimization_barrier(jnp.sum(key_grads.reshape(kv_count, group_size, length, head_width), axis=1))[:, places]
        value_sum = lax.optimization_barrier(jnp.sum(value_grads.reshape(kv_count, group_size, length, head_width), axis=1))[:, places]
        key_list.append(jnp.transpose(key_sum, (1, 0, 2)))
        value_list.append(jnp.transpose(value_sum, (1, 0, 2)))
    attended = jnp.stack(attended_list)
    grad_query = jnp.stack(query_list)
    grad_key_value = jnp.stack([jnp.stack(key_list), jnp.stack(value_list)]).astype(jnp.bfloat16)
    return (attended, grad_query, grad_key_value)
```

```python
import functools
import math

import jax
import jax.numpy as jnp
from jax import lax
from jax.experimental import pallas as pl
from jax.experimental.pallas import tpu as pltpu
from jax.sharding import PartitionSpec as P

HIDDEN = -1e30
CHUNK_TOKENS = 16
F32 = jnp.float32
BF16 = jnp.bfloat16


def dot(left, right):
    return lax.dot_general(left, right, (((1,), (0,)), ((), ())), preferred_element_type=F32)


def dot_t(left, right):
    return lax.dot_general(left, right, (((1,), (1,)), ((), ())), preferred_element_type=F32)


def dot_l(left, right):
    return lax.dot_general(left, right, (((0,), (0,)), ((), ())), preferred_element_type=F32)


def kernel(
    sizes,
    q_hbm, kv_hbm, g_hbm, doc_hbm, order_hbm, mask_hbm,
    att_hbm, dq_hbm, dkv_hbm,
    q_ref, kv_ref, g_ref, doc_ref, order_ref, mask_ref,
    att_ref, dq_ref, dkv_ref,
    kvs, counts, dcounts, pieces, staged, landed, heads_ref,
    e_ref, po_ref, dpo_ref, atto_ref, pmo_ref, dso_ref, pp_ref, pmp_ref, dsp_ref,
    local_sem, kv_send, kv_recv, count_send, count_recv, dcount_send, dcount_recv,
    grad_send, grad_recv, head_send, head_recv,
):
    n, nd, nt, rows, heads, width, window, tail, docs, part_chunks, weight_top = sizes
    me = lax.axis_index("ctx")
    my_dp = lax.axis_index("dp")
    my_head = lax.axis_index("tensor")
    chunk = CHUNK_TOKENS * heads
    chunks = rows // CHUNK_TOKENS
    skip = rows - tail
    factor = 1.0 / math.sqrt(width)
    steep = factor * math.log2(math.e)

    barrier = pltpu.get_barrier_semaphore()
    for axis, mine, count in (("ctx", me, n), ("dp", my_dp, nd), ("tensor", my_head, nt)):
        for step in range(1, count):
            pl.semaphore_signal(
                barrier,
                inc=1,
                device_id={axis: lax.rem(mine + step, count)},
                device_id_type=pl.DeviceIdType.MESH,
            )

    loads = [
        pltpu.make_async_copy(source, target, local_sem.at[i])
        for i, (source, target) in enumerate(
            (
                (kv_hbm, kv_ref),
                (mask_hbm, mask_ref),
                (doc_hbm, doc_ref),
                (order_hbm, order_ref),
                (q_hbm, q_ref),
                (g_hbm, g_ref),
            )
        )
    ]
    for load in loads:
        load.start()

    def remote(source, target, send, recv, axis, mine, count, step):
        return pltpu.make_async_remote_copy(
            src_ref=source,
            dst_ref=target,
            send_sem=send.at[step],
            recv_sem=recv.at[step],
            device_id={axis: lax.rem(mine + step, count)},
            device_id_type=pl.DeviceIdType.MESH,
        )

    gap = lax.broadcasted_iota(jnp.int32, (chunk, rows), 0) - heads * lax.broadcasted_iota(
        jnp.int32, (chunk, rows), 1
    )
    for c in range(chunks):
        moved = gap + c * chunk
        e_ref[c] = jnp.where((moved >= 0) & (moved < heads), 1.0, 0.0).astype(BF16)
    pick = (
        lax.broadcasted_iota(jnp.int32, (rows, rows * nt), 1)
        - nt * lax.broadcasted_iota(jnp.int32, (rows, rows * nt), 0)
    )
    own_pick = jnp.where(pick == my_head, 1.0, 0.0).astype(BF16)

    loads[0].wait()
    k_own = dot(own_pick, kv_ref[0]).astype(BF16)
    v_own = dot(own_pick, kv_ref[1]).astype(BF16)
    kvs[me, 0] = k_own[skip:]
    kvs[me, 1] = v_own[skip:]
    loads[1].wait()
    counts[me] = mask_ref[...]
    pl.semaphore_wait(barrier, n + nd + nt - 3)
    kv_copies = [
        remote(kvs.at[me], kvs.at[me], kv_send, kv_recv, "ctx", me, n, step)
        for step in range(1, n)
    ]
    for copy in kv_copies:
        copy.start()
    count_copies = [
        remote(counts.at[me], counts.at[me], count_send, count_recv, "ctx", me, n, step)
        for step in range(1, n)
    ]
    for copy in count_copies:
        copy.start()

    loads[2].wait()
    loads[3].wait()
    own = order_ref[0, me]
    token_row = lax.broadcasted_iota(jnp.int32, (1, rows), 1)
    place_row = own * rows + token_row
    start_row = jnp.zeros((1, rows), jnp.int32)
    bound = jnp.int32(0)
    for j in range(docs):
        bound = bound + doc_ref[0, j]
        start_row = jnp.where(bound <= place_row, bound, start_row)
    key_rows = lax.broadcasted_iota(jnp.int32, (rows, rows), 0)

    def bias_of(target):
        key_places = target * rows + key_rows
        seen = (key_places >= start_row) & (key_places <= place_row)
        return jnp.where(seen, 0.0, HIDDEN).astype(BF16)

    def flipped(block):
        return jnp.transpose(block.astype(F32)).astype(BF16)

    wide_own = jnp.concatenate([k_own, bias_of(own)], axis=1)
    kt_own = flipped(k_own)
    vt_own = flipped(v_own)
    mask_rows = jnp.broadcast_to(mask_ref[...].astype(F32), (8, rows)).astype(BF16)

    def cols(c):
        return pl.ds(c * chunk, chunk)

    def wide_queries(c):
        return jnp.concatenate([q_ref[cols(c), :], e_ref[c]], axis=1)

    loads[4].wait()
    loads[5].wait()
    top, total, drift, kept = [], [], [], []

    def close_own(c, gain, delta):
        masked = po_ref[:, cols(c)] * gain
        pmo_ref[:, cols(c)] = masked.astype(BF16)
        dso_ref[:, cols(c)] = (masked * (dpo_ref[:, cols(c)] - delta)).astype(BF16)

    for c in range(chunks):
        scores = dot_t(wide_own, wide_queries(c))
        grads = dot_t(v_own, g_ref[cols(c), :])
        highest = jnp.max(scores, axis=0, keepdims=True)
        raised = jnp.exp2((scores - highest) * steep)
        summed = jnp.sum(raised, axis=0, keepdims=True)
        drifted = jnp.sum(raised * grads, axis=0, keepdims=True)
        top.append(highest)
        total.append(summed)
        drift.append(drifted)
        kept.append(dot_t(mask_rows, e_ref[c])[0:1])
        po_ref[:, cols(c)] = raised
        dpo_ref[:, cols(c)] = grads
        own_part = dot(vt_own, raised.astype(BF16))
        if c < part_chunks:
            atto_ref[:, cols(c)] = own_part
        else:
            inverse = 1.0 / summed
            close_own(c, kept[c] * inverse, drifted * inverse)
            att_ref[cols(c), :] = jnp.transpose(own_part * inverse).astype(BF16)

    for copy in kv_copies:
        copy.wait()
    for copy in count_copies:
        copy.wait()
    dcounts[my_dp] = jnp.sum(counts[...], axis=0)
    dcount_copies = [
        remote(dcounts.at[my_dp], dcounts.at[my_dp], dcount_send, dcount_recv, "dp", my_dp, nd, step)
        for step in range(1, nd)
    ]
    for copy in dcount_copies:
        copy.start()
    targets, wide, values, kts, vts = [], [], [], [], []
    for w in range(window):
        target = own - 1 - w
        holder = jnp.int32(0)
        for j in range(n):
            holder = holder + jnp.where(order_ref[0, j] == target, j, 0)
        pair = kvs[holder]
        empty = jnp.zeros((skip, width), BF16)
        block_k = jnp.concatenate([empty, pair[0]], axis=0) if skip else pair[0]
        block_v = jnp.concatenate([empty, pair[1]], axis=0) if skip else pair[1]
        targets.append(target)
        wide.append(jnp.concatenate([block_k, bias_of(target)], axis=1))
        values.append(block_v)
        kts.append(flipped(block_k))
        vts.append(flipped(block_v))

    gains, deltas, inverses, fades = [], [], [], []
    for c in range(part_chunks):
        queries = wide_queries(c)
        scores = [dot_t(wide[w], queries) for w in range(window)]
        grads = [dot_t(values[w], g_ref[cols(c), :]) for w in range(window)]
        highest = top[c]
        for w in range(window):
            highest = jnp.maximum(highest, jnp.max(scores[w], axis=0, keepdims=True))
        fade = jnp.exp2((top[c] - highest) * steep)
        summed = total[c] * fade
        drifted = drift[c] * fade
        raised = []
        for w in range(window):
            part = jnp.exp2((scores[w] - highest) * steep)
            summed = summed + jnp.sum(part, axis=0, keepdims=True)
            drifted = drifted + jnp.sum(part * grads[w], axis=0, keepdims=True)
            pp_ref[w, :, cols(c)] = part.astype(BF16)
            raised.append(part)
        inverse = 1.0 / summed
        delta = drifted * inverse
        gain = kept[c] * inverse
        for w in range(window):
            masked = raised[w] * gain
            pmp_ref[w, :, cols(c)] = masked.astype(BF16)
            dsp_ref[w, :, cols(c)] = (masked * (grads[w] - delta)).astype(BF16)
        gains.append(gain * fade)
        deltas.append(delta)
        inverses.append(inverse)
        fades.append(fade)

    part_rows = part_chunks * chunk
    for w in range(window):
        pieces[w, 0] = (dot(dsp_ref[w], q_ref[:part_rows, :])[skip:] * factor).astype(BF16)
        pieces[w, 1] = dot(pmp_ref[w], g_ref[:part_rows, :])[skip:].astype(BF16)
    pieces[window] = jnp.zeros((2, tail, width), BF16)
    grad_copies = []
    for step in range(1, n):
        peer = lax.rem(me + step, n)
        chosen = jnp.int32(window)
        for w in range(window):
            chosen = jnp.where(order_ref[0, peer] == targets[w], w, chosen)
        staged[step] = pieces[chosen]
        copy = remote(staged.at[step], landed.at[step], grad_send, grad_recv, "ctx", me, n, step)
        copy.start()
        grad_copies.append(copy)

    for c in range(part_chunks):
        close_own(c, gains[c], deltas[c])
        both = atto_ref[:, cols(c)] * fades[c]
        for w in range(window):
            both = both + dot(vts[w], pp_ref[w, :, cols(c)])
        att_ref[cols(c), :] = jnp.transpose(both * inverses[c]).astype(BF16)
    att_out = pltpu.make_async_copy(att_ref, att_hbm, local_sem.at[6])
    att_out.start()
    own_k = dot(dso_ref[...], q_ref[...]) * factor
    own_v = dot(pmo_ref[...], g_ref[...])
    for copy in dcount_copies:
        copy.wait()
    counted = jnp.sum(
        jnp.sum(dcounts[...], axis=0).astype(F32), axis=1, keepdims=True
    )
    weight = weight_top / jnp.maximum(counted, 1.0)
    for c in range(chunks):
        back = dot(kt_own, dso_ref[:, cols(c)])
        if c < part_chunks:
            for w in range(window):
                back = back + dot(kts[w], dsp_ref[w, :, cols(c)])
        dq_ref[cols(c), :] = jnp.transpose(back * (weight * factor)).astype(BF16)
    dq_out = pltpu.make_async_copy(dq_ref, dq_hbm, local_sem.at[7])
    dq_out.start()

    for copy in grad_copies:
        copy.wait()
    arrived_k = landed[1, 0].astype(F32)
    arrived_v = landed[1, 1].astype(F32)
    for step in range(2, n):
        arrived_k = arrived_k + landed[step, 0].astype(F32)
        arrived_v = arrived_v + landed[step, 1].astype(F32)
    if skip:
        clear = jnp.zeros((skip, width), F32)
        arrived_k = jnp.concatenate([clear, arrived_k], axis=0)
        arrived_v = jnp.concatenate([clear, arrived_v], axis=0)
    heads_ref[my_head, 0] = ((own_k + arrived_k) * weight).astype(BF16)
    heads_ref[my_head, 1] = ((own_v + arrived_v) * weight).astype(BF16)
    head_copies = [
        remote(heads_ref.at[my_head], heads_ref.at[my_head], head_send, head_recv, "tensor", my_head, nt, step)
        for step in range(1, nt)
    ]
    for copy in head_copies:
        copy.start()
    for copy in head_copies:
        copy.wait()
    for i in range(2):
        mixed = None
        for h in range(nt):
            spread = jnp.where(pick == h, 1.0, 0.0).astype(BF16)
            term = dot_l(spread, heads_ref[h, i])
            mixed = term if mixed is None else mixed + term
        dkv_ref[i] = mixed.astype(BF16)
    dkv_out = pltpu.make_async_copy(dkv_ref, dkv_hbm, local_sem.at[8])
    dkv_out.start()
    att_out.wait()
    dq_out.wait()
    dkv_out.wait()


def local(query, key_value, grad_out, doc_lengths, stretch_order, loss_mask):
    _, rows, heads, width = query.shape
    n, nd, nt = lax.axis_size("ctx"), lax.axis_size("dp"), lax.axis_size("tensor")
    length = rows * n
    longest = length * 5 // 32
    window = (longest - 1 + rows - 1) // rows
    tail = rows if window > 1 else -(-(longest - 1) // 16) * 16
    reach = min(rows, longest - 1 + rows - rows * 1) if window == 1 else rows
    part_chunks = min(rows // CHUNK_TOKENS, -(-reach // CHUNK_TOKENS))
    docs = doc_lengths.shape[1]
    total = rows * heads
    part = part_chunks * CHUNK_TOKENS * heads
    chunk = CHUNK_TOKENS * heads
    chunks = rows // CHUNK_TOKENS
    weight_top = float(nd * query.shape[0] * length)
    sizes = (n, nd, nt, rows, heads, width, window, tail, docs, part_chunks, weight_top)
    dma = pltpu.SemaphoreType.DMA
    any_spec = pl.BlockSpec(memory_space=pl.ANY)
    att, dq, dkv = pl.pallas_call(
        functools.partial(kernel, sizes),
        out_shape=(
            jax.ShapeDtypeStruct((total, width), BF16),
            jax.ShapeDtypeStruct((total, width), BF16),
            jax.ShapeDtypeStruct((2, rows * nt, width), BF16),
        ),
        in_specs=[any_spec] * 6,
        out_specs=(any_spec,) * 3,
        scratch_shapes=[
            pltpu.VMEM((total, width), BF16),
            pltpu.VMEM((2, rows * nt, width), BF16),
            pltpu.VMEM((total, width), BF16),
            pltpu.SMEM((1, docs), jnp.int32),
            pltpu.SMEM((1, n), jnp.int32),
            pltpu.VMEM((1, rows), jnp.int32),
            pltpu.VMEM((total, width), BF16),
            pltpu.VMEM((total, width), BF16),
            pltpu.VMEM((2, rows * nt, width), BF16),
            pltpu.VMEM((n, 2, tail, width), BF16),
            pltpu.VMEM((n, 1, rows), jnp.int32),
            pltpu.VMEM((nd, 1, rows), jnp.int32),
            pltpu.VMEM((window + 1, 2, tail, width), BF16),
            pltpu.VMEM((n, 2, tail, width), BF16),
            pltpu.VMEM((n, 2, tail, width), BF16),
            pltpu.VMEM((nt, 2, rows, width), BF16),
            pltpu.VMEM((chunks, chunk, rows), BF16),
            pltpu.VMEM((rows, total), F32),
            pltpu.VMEM((rows, total), F32),
            pltpu.VMEM((width, part), F32),
            pltpu.VMEM((rows, total), BF16),
            pltpu.VMEM((rows, total), BF16),
            pltpu.VMEM((window, rows, part), BF16),
            pltpu.VMEM((window, rows, part), BF16),
            pltpu.VMEM((window, rows, part), BF16),
            dma((9,)),
            dma((n,)), dma((n,)),
            dma((n,)), dma((n,)),
            dma((nd,)), dma((nd,)),
            dma((n,)), dma((n,)),
            dma((nt,)), dma((nt,)),
        ],
        compiler_params=pltpu.CompilerParams(collective_id=0, has_side_effects=True),
        name="packed_attention",
    )(
        query.reshape(total, width),
        key_value.reshape(2, rows * nt, width),
        grad_out.reshape(total, width),
        doc_lengths,
        stretch_order,
        loss_mask,
    )
    return (
        att.reshape(query.shape),
        dq.reshape(query.shape),
        dkv.reshape(key_value.shape),
    )


def solution(mesh):
    placed = (
        P("dp", "ctx", "tensor", None),
        P(None, "dp", "ctx", None, None),
        P("dp", "ctx", "tensor", None),
        P("dp", None),
        P("dp", None),
        P("dp", "ctx"),
    )
    return jax.shard_map(
        local,
        mesh=mesh,
        in_specs=placed,
        out_specs=(
            P("dp", "ctx", "tensor", None),
            P("dp", "ctx", "tensor", None),
            P(None, "dp", "ctx", None, None),
        ),
        check_vma=False,
    )
```

```python
import functools
import math

import jax
import jax.numpy as jnp
from jax import lax
from jax.experimental import pallas as pl
from jax.experimental.pallas import tpu as pltpu
from jax.sharding import PartitionSpec as P

HIDDEN = -1e30
CHUNK_TOKENS = 16
KERNEL_VMEM = 32 * 1024 * 1024
F32 = jnp.float32
BF16 = jnp.bfloat16


def dot(left, right):
    return lax.dot_general(left, right, (((1,), (0,)), ((), ())), preferred_element_type=F32)


def dot_t(left, right):
    return lax.dot_general(left, right, (((1,), (1,)), ((), ())), preferred_element_type=F32)


def dot_l(left, right):
    return lax.dot_general(left, right, (((0,), (0,)), ((), ())), preferred_element_type=F32)


def kernel(
    sizes,
    q_hbm, kv_hbm, g_hbm, doc_hbm, order_hbm, mask_hbm,
    att_ref, dq_ref, dkv_ref,
    q_ref, kv_ref, g_ref, doc_ref, order_ref, mask_ref,
    k_all, v_all, counts, dcounts, pieces, staged, landed, owns, tails, base, spread,
    e_ref, po_ref, dpo_ref, atto_ref, pmo_ref, dso_ref, pf_ref, pmp_ref, dsp_ref,
    local_sem, kv_send, kv_recv, count_send, count_recv, dcount_send, dcount_recv,
    grad_send, grad_recv, own_send, own_recv, tail_send, tail_recv,
):
    n, nd, nt, rows, heads, width, window, tail, docs, part_chunks, weight_top = sizes
    me = lax.axis_index("ctx")
    my_dp = lax.axis_index("dp")
    my_head = lax.axis_index("tensor")
    chunk = CHUNK_TOKENS * heads
    chunks = rows // CHUNK_TOKENS
    part_rows = part_chunks * chunk
    skip = rows - tail
    factor = 1.0 / math.sqrt(width)
    steep = factor * math.log2(math.e)

    barrier = pltpu.get_barrier_semaphore()
    for axis, mine, count in (("ctx", me, n), ("dp", my_dp, nd), ("tensor", my_head, nt)):
        for step in range(1, count):
            pl.semaphore_signal(
                barrier,
                inc=1,
                device_id={axis: lax.rem(mine + step, count)},
                device_id_type=pl.DeviceIdType.MESH,
            )

    loads = [
        pltpu.make_async_copy(source, target, local_sem.at[i])
        for i, (source, target) in enumerate(
            (
                (kv_hbm, kv_ref),
                (mask_hbm, mask_ref),
                (doc_hbm, doc_ref),
                (order_hbm, order_ref),
                (q_hbm, q_ref),
                (g_hbm, g_ref),
            )
        )
    ]
    for load in loads:
        load.start()

    upper = (2 * me) // n
    short = me + upper * (n - 1 - 2 * me)
    spare = n - 1 - 2 * short
    side = 1 - 2 * upper
    far_first = []
    for k in range(n - 1):
        paired = k - spare
        distance = jnp.where(paired < 0, n - 1 - short - k, short - paired // 2)
        turn = jnp.where(paired < 0, 1, 1 - 2 * (paired % 2))
        far_first.append(me + side * turn * distance)

    def remote(source, target, send, recv, axis, peer):
        return pltpu.make_async_remote_copy(
            src_ref=source,
            dst_ref=target,
            send_sem=send,
            recv_sem=recv,
            device_id={axis: peer},
            device_id_type=pl.DeviceIdType.MESH,
        )

    gap = lax.broadcasted_iota(jnp.int32, (chunk, rows), 0) - heads * lax.broadcasted_iota(
        jnp.int32, (chunk, rows), 1
    )
    for c in range(chunks):
        moved = gap + c * chunk
        e_ref[c] = jnp.where((moved >= 0) & (moved < heads), 1.0, 0.0).astype(BF16)
    pick = (
        lax.broadcasted_iota(jnp.int32, (rows, rows * nt), 1)
        - nt * lax.broadcasted_iota(jnp.int32, (rows, rows * nt), 0)
    )
    own_pick = jnp.where(pick == my_head, 1.0, 0.0).astype(BF16)

    loads[0].wait()
    k_own = dot(own_pick, kv_ref[0]).astype(BF16)
    k_all[me] = k_own[skip:]
    v_own = dot(own_pick, kv_ref[1]).astype(BF16)
    v_all[me] = v_own[skip:]
    loads[1].wait()
    counts[me] = mask_ref[...]
    pl.semaphore_wait(barrier, n + nd + nt - 3)

    def kv_copy(i, source, peer):
        held = (k_all, v_all)[i]
        return remote(
            held.at[me], held.at[source], kv_send.at[i, peer], kv_recv.at[i, source], "ctx", peer
        )

    def count_copy(source, peer):
        return remote(
            counts.at[me], counts.at[source], count_send.at[peer], count_recv.at[source], "ctx", peer
        )

    for peer in far_first:
        kv_copy(0, me, peer).start()
    for peer in far_first:
        kv_copy(1, me, peer).start()
    for peer in far_first:
        count_copy(me, peer).start()

    loads[2].wait()
    loads[3].wait()
    own = order_ref[0, me]
    token_row = lax.broadcasted_iota(jnp.int32, (1, rows), 1)
    place_row = own * rows + token_row
    start_row = jnp.zeros((1, rows), jnp.int32)
    bound = jnp.int32(0)
    for j in range(docs):
        bound = bound + doc_ref[0, j]
        start_row = jnp.where(bound <= place_row, bound, start_row)
    key_rows = lax.broadcasted_iota(jnp.int32, (rows, rows), 0)

    def bias_of(target):
        key_places = target * rows + key_rows
        seen = (key_places >= start_row) & (key_places <= place_row)
        return jnp.where(seen, 0.0, HIDDEN).astype(BF16)

    def flipped(block):
        return jnp.transpose(block.astype(F32)).astype(BF16)

    wide_own = jnp.concatenate([k_own, bias_of(own)], axis=1)
    kt_own = flipped(k_own)
    vt_own = flipped(v_own)
    mask_rows = jnp.broadcast_to(mask_ref[...].astype(F32), (8, rows)).astype(BF16)
    turned = lax.broadcasted_iota(jnp.int32, (rows * nt, rows), 0) - nt * lax.broadcasted_iota(
        jnp.int32, (rows * nt, rows), 1
    )
    for h in range(nt):
        spread[h] = jnp.where(turned == h, 1.0, 0.0).astype(BF16)

    def cols(c):
        return pl.ds(c * chunk, chunk)

    def wide_queries(c):
        return jnp.concatenate([q_ref[cols(c), :], e_ref[c]], axis=1)

    loads[4].wait()
    loads[5].wait()
    top, total, drift, kept = [], [], [], []

    def close_own(c, gain, delta):
        masked = po_ref[:, cols(c)] * gain
        pmo_ref[:, cols(c)] = masked.astype(BF16)
        dso_ref[:, cols(c)] = (masked * (dpo_ref[:, cols(c)] - delta)).astype(BF16)

    for c in range(chunks):
        scores = dot_t(wide_own, wide_queries(c))
        grads = dot_t(v_own, g_ref[cols(c), :])
        highest = jnp.max(scores, axis=0, keepdims=True)
        raised = jnp.exp2((scores - highest) * steep)
        summed = jnp.sum(raised, axis=0, keepdims=True)
        drifted = jnp.sum(raised * grads, axis=0, keepdims=True)
        top.append(highest)
        total.append(summed)
        drift.append(drifted)
        kept.append(dot_t(mask_rows, e_ref[c])[0:1])
        po_ref[:, cols(c)] = raised
        dpo_ref[:, cols(c)] = grads
        own_part = dot(vt_own, raised.astype(BF16))
        if c < part_chunks:
            atto_ref[:, cols(c)] = own_part
        else:
            inverse = 1.0 / summed
            close_own(c, kept[c] * inverse, drifted * inverse)
            att_ref[cols(c), :] = jnp.transpose(own_part * inverse).astype(BF16)

    def others():
        return [lax.rem(me + step, n) for step in range(1, n)]

    def filled(block):
        if not skip:
            return block
        return jnp.concatenate([jnp.zeros((skip, width), block.dtype), block], axis=0)

    def grad_copy(i, step):
        return remote(
            staged.at[i, step],
            landed.at[i, step],
            grad_send.at[i, step],
            grad_recv.at[i, step],
            "ctx",
            lax.rem(me + step, n),
        )

    def scatter(i):
        pieces[i, window] = jnp.zeros((tail, width), BF16)
        for step in range(1, n):
            peer = lax.rem(me + step, n)
            chosen = jnp.int32(window)
            for w in range(window):
                chosen = jnp.where(order_ref[0, peer] == targets[w], w, chosen)
            staged[i, step] = pieces[i, chosen]
        for peer in far_first:
            grad_copy(i, lax.rem(peer - me + n, n)).start()

    for peer in others():
        kv_copy(0, peer, peer).wait()
    targets = [own - 1 - w for w in range(window)]
    holders = []
    for w in range(window):
        holder = jnp.int32(0)
        for j in range(n):
            holder = holder + jnp.where(order_ref[0, j] == targets[w], j, 0)
        holders.append(holder)
    keys = [filled(k_all[holders[w]]) for w in range(window)]
    wide = [jnp.concatenate([keys[w], bias_of(targets[w])], axis=1) for w in range(window)]
    gains, inverses, fades = [], [], []
    for c in range(part_chunks):
        queries = wide_queries(c)
        scores = [dot_t(wide[w], queries) for w in range(window)]
        highest = top[c]
        for w in range(window):
            highest = jnp.maximum(highest, jnp.max(scores[w], axis=0, keepdims=True))
        fade = jnp.exp2((top[c] - highest) * steep)
        summed = total[c] * fade
        raised = []
        for w in range(window):
            part = jnp.exp2((scores[w] - highest) * steep)
            summed = summed + jnp.sum(part, axis=0, keepdims=True)
            pf_ref[w, :, cols(c)] = part
            raised.append(part)
        inverse = 1.0 / summed
        gain = kept[c] * inverse
        for w in range(window):
            pmp_ref[w, :, cols(c)] = (raised[w] * gain).astype(BF16)
        gains.append(gain)
        inverses.append(inverse)
        fades.append(fade)
    for w in range(window):
        pieces[1, w] = dot(pmp_ref[w], g_ref[:part_rows, :])[skip:].astype(BF16)
    scatter(1)

    for peer in others():
        kv_copy(1, peer, peer).wait()
    values = [filled(v_all[holders[w]]) for w in range(window)]
    deltas = []
    for c in range(part_chunks):
        grads = [dot_t(values[w], g_ref[cols(c), :]) for w in range(window)]
        raised = [pf_ref[w, :, cols(c)] for w in range(window)]
        drifted = drift[c] * fades[c]
        for w in range(window):
            drifted = drifted + jnp.sum(raised[w] * grads[w], axis=0, keepdims=True)
        delta = drifted * inverses[c]
        for w in range(window):
            dsp_ref[w, :, cols(c)] = (raised[w] * gains[c] * (grads[w] - delta)).astype(BF16)
        deltas.append(delta)
    for w in range(window):
        pieces[0, w] = (dot(dsp_ref[w], q_ref[:part_rows, :])[skip:] * factor).astype(BF16)
    scatter(0)

    for peer in others():
        count_copy(peer, peer).wait()
    dcounts[my_dp] = jnp.sum(counts[...], axis=0)
    dcount_copies = [
        remote(
            dcounts.at[my_dp],
            dcounts.at[my_dp],
            dcount_send.at[step],
            dcount_recv.at[step],
            "dp",
            lax.rem(my_dp + step, nd),
        )
        for step in range(1, nd)
    ]
    for copy in dcount_copies:
        copy.start()

    def head_copies(buffer, send, recv):
        return [
            remote(
                buffer.at[my_head],
                buffer.at[my_head],
                send.at[step],
                recv.at[step],
                "tensor",
                lax.rem(my_head + step, nt),
            )
            for step in range(1, nt)
        ]

    for c in range(part_chunks):
        close_own(c, gains[c] * fades[c], deltas[c])
    owns[my_head, 0] = (dot(dso_ref[...], q_ref[...]) * factor).astype(BF16)
    owns[my_head, 1] = dot(pmo_ref[...], g_ref[...]).astype(BF16)
    own_copies = head_copies(owns, own_send, own_recv)
    for copy in own_copies:
        copy.start()

    vts = [flipped(values[w]) for w in range(window)]
    for c in range(part_chunks):
        both = atto_ref[:, cols(c)] * fades[c]
        for w in range(window):
            both = both + dot(vts[w], pf_ref[w, :, cols(c)].astype(BF16))
        att_ref[cols(c), :] = jnp.transpose(both * inverses[c]).astype(BF16)

    def forward(i):
        for step in range(1, n):
            grad_copy(i, step).wait()
        arrived = landed[i, 1].astype(F32)
        for step in range(2, n):
            arrived = arrived + landed[i, step].astype(F32)
        tails[i, my_head] = arrived.astype(BF16)
        copies = head_copies(tails.at[i], tail_send.at[i], tail_recv.at[i])
        for copy in copies:
            copy.start()
        return copies

    tail_v = forward(1)
    for copy in dcount_copies:
        copy.wait()
    counted = jnp.sum(
        jnp.sum(dcounts[...], axis=0).astype(F32), axis=1, keepdims=True
    )
    weight = weight_top / jnp.maximum(counted, 1.0)
    kts = [flipped(keys[w]) for w in range(window)]
    for c in range(chunks):
        back = dot(kt_own, dso_ref[:, cols(c)])
        if c < part_chunks:
            for w in range(window):
                back = back + dot(kts[w], dsp_ref[w, :, cols(c)])
        dq_ref[cols(c), :] = jnp.transpose(back * (weight * factor)).astype(BF16)

    def mixed(blocks):
        result = dot(spread[0], blocks[0])
        for h in range(1, nt):
            result = result + dot(spread[h], blocks[h])
        return result

    for copy in own_copies:
        copy.wait()
    for i in range(2):
        base[i] = mixed([owns[h, i] for h in range(nt)])

    def finish(i, copies):
        for copy in copies:
            copy.wait()
        arrived = mixed([filled(tails[i, h]) for h in range(nt)])
        dkv_ref[i] = ((base[i] + arrived) * weight).astype(BF16)

    tail_k = forward(0)
    finish(1, tail_v)
    finish(0, tail_k)


def write_out(att_ref, dq_ref, dkv_ref, att_hbm, dq_hbm, dkv_hbm, sems):
    copies = [
        pltpu.make_async_copy(source, target, sems.at[i])
        for i, (source, target) in enumerate(
            ((dkv_ref, dkv_hbm), (att_ref, att_hbm), (dq_ref, dq_hbm))
        )
    ]
    for copy in copies:
        copy.start()
    for copy in copies:
        copy.wait()


def local(query, key_value, grad_out, doc_lengths, stretch_order, loss_mask):
    _, rows, heads, width = query.shape
    n, nd, nt = lax.axis_size("ctx"), lax.axis_size("dp"), lax.axis_size("tensor")
    length = rows * n
    longest = length * 5 // 32
    window = (longest - 1 + rows - 1) // rows
    tail = rows if window > 1 else -(-(longest - 1) // 16) * 16
    reach = min(rows, longest - 1) if window == 1 else rows
    part_chunks = min(rows // CHUNK_TOKENS, -(-reach // CHUNK_TOKENS))
    docs = doc_lengths.shape[1]
    total = rows * heads
    part = part_chunks * CHUNK_TOKENS * heads
    chunk = CHUNK_TOKENS * heads
    chunks = rows // CHUNK_TOKENS
    weight_top = float(nd * query.shape[0] * length)
    sizes = (n, nd, nt, rows, heads, width, window, tail, docs, part_chunks, weight_top)
    dma = pltpu.SemaphoreType.DMA
    any_spec = pl.BlockSpec(memory_space=pl.ANY)
    vmem_spec = pl.BlockSpec(memory_space=pltpu.VMEM)
    shapes = (
        jax.ShapeDtypeStruct((total, width), BF16),
        jax.ShapeDtypeStruct((total, width), BF16),
        jax.ShapeDtypeStruct((2, rows * nt, width), BF16),
    )
    results = pl.pallas_call(
        functools.partial(kernel, sizes),
        out_shape=shapes,
        in_specs=[pl.BlockSpec(memory_space=pltpu.MemorySpace.HBM)] * 6,
        out_specs=(vmem_spec,) * 3,
        scratch_shapes=[
            pltpu.VMEM((total, width), BF16),
            pltpu.VMEM((2, rows * nt, width), BF16),
            pltpu.VMEM((total, width), BF16),
            pltpu.SMEM((1, docs), jnp.int32),
            pltpu.SMEM((1, n), jnp.int32),
            pltpu.VMEM((1, rows), jnp.int32),
            pltpu.VMEM((n, tail, width), BF16),
            pltpu.VMEM((n, tail, width), BF16),
            pltpu.VMEM((n, 1, rows), jnp.int32),
            pltpu.VMEM((nd, 1, rows), jnp.int32),
            pltpu.VMEM((2, window + 1, tail, width), BF16),
            pltpu.VMEM((2, n, tail, width), BF16),
            pltpu.VMEM((2, n, tail, width), BF16),
            pltpu.VMEM((nt, 2, rows, width), BF16),
            pltpu.VMEM((2, nt, tail, width), BF16),
            pltpu.VMEM((2, rows * nt, width), F32),
            pltpu.VMEM((nt, rows * nt, rows), BF16),
            pltpu.VMEM((chunks, chunk, rows), BF16),
            pltpu.VMEM((rows, total), F32),
            pltpu.VMEM((rows, total), F32),
            pltpu.VMEM((width, part), F32),
            pltpu.VMEM((rows, total), BF16),
            pltpu.VMEM((rows, total), BF16),
            pltpu.VMEM((window, rows, part), F32),
            pltpu.VMEM((window, rows, part), BF16),
            pltpu.VMEM((window, rows, part), BF16),
            dma((6,)),
            dma((2, n)), dma((2, n)),
            dma((n,)), dma((n,)),
            dma((nd,)), dma((nd,)),
            dma((2, n)), dma((2, n)),
            dma((nt,)), dma((nt,)),
            dma((2, nt)), dma((2, nt)),
        ],
        compiler_params=pltpu.CompilerParams(
            collective_id=0, has_side_effects=True, vmem_limit_bytes=KERNEL_VMEM
        ),
        name="packed_attention",
    )(
        *(
            pltpu.with_memory_space_constraint(array, pltpu.MemorySpace.HBM)
            for array in (
                query.reshape(total, width),
                key_value.reshape(2, rows * nt, width),
                grad_out.reshape(total, width),
                doc_lengths,
                stretch_order,
                loss_mask,
            )
        )
    )
    att, dq, dkv = pl.pallas_call(
        write_out,
        out_shape=shapes,
        in_specs=[vmem_spec] * 3,
        out_specs=(any_spec,) * 3,
        scratch_shapes=[dma((3,))],
        compiler_params=pltpu.CompilerParams(vmem_limit_bytes=KERNEL_VMEM),
        name="write_out",
    )(*results)
    return (
        att.reshape(query.shape),
        dq.reshape(query.shape),
        dkv.reshape(key_value.shape),
    )


def solution(mesh):
    placed = (
        P("dp", "ctx", "tensor", None),
        P(None, "dp", "ctx", None, None),
        P("dp", "ctx", "tensor", None),
        P("dp", None),
        P("dp", None),
        P("dp", "ctx"),
    )
    return jax.shard_map(
        local,
        mesh=mesh,
        in_specs=placed,
        out_specs=(
            P("dp", "ctx", "tensor", None),
            P("dp", "ctx", "tensor", None),
            P(None, "dp", "ctx", None, None),
        ),
        check_vma=False,
    )
```

```python
import functools
import math

import jax
import jax.numpy as jnp
from jax import lax
from jax.experimental import pallas as pl
from jax.experimental.pallas import tpu as pltpu
from jax.sharding import PartitionSpec as P

HIDDEN = -1e30
CHUNK_TOKENS = 16
KERNEL_VMEM = 32 * 1024 * 1024
OUT_PIECES = 4
F32 = jnp.float32
BF16 = jnp.bfloat16


def dot(left, right):
    return lax.dot_general(left, right, (((1,), (0,)), ((), ())), preferred_element_type=F32)


def dot_t(left, right):
    return lax.dot_general(left, right, (((1,), (1,)), ((), ())), preferred_element_type=F32)


def dot_l(left, right):
    return lax.dot_general(left, right, (((0,), (0,)), ((), ())), preferred_element_type=F32)


def kernel(
    sizes,
    q_hbm, kv_hbm, g_hbm, doc_hbm, order_hbm, mask_hbm,
    att_ref, dq_ref, dkv_ref,
    q_ref, kv_ref, g_ref, doc_ref, order_ref, mask_ref,
    k_all, v_all, counts, dcounts, pieces, staged, landed, owns, tails, base, spread,
    e_ref, po_ref, dpo_ref, atto_ref, pmo_ref, dso_ref, pf_ref, pmp_ref, dsp_ref,
    local_sem, kv_send, kv_recv, count_send, count_recv, dcount_send, dcount_recv,
    grad_send, grad_recv, own_send, own_recv, tail_send, tail_recv,
):
    n, nd, nt, rows, heads, width, window, tail, docs, longest, part_chunks, weight_top = sizes
    me = lax.axis_index("ctx")
    my_dp = lax.axis_index("dp")
    my_head = lax.axis_index("tensor")
    chunk = CHUNK_TOKENS * heads
    chunks = rows // CHUNK_TOKENS
    part_rows = part_chunks * chunk
    skip = rows - tail
    factor = 1.0 / math.sqrt(width)
    steep = factor * math.log2(math.e)

    barrier = pltpu.get_barrier_semaphore()
    for axis, mine, count in (("ctx", me, n), ("dp", my_dp, nd), ("tensor", my_head, nt)):
        for step in range(1, count):
            pl.semaphore_signal(
                barrier,
                inc=1,
                device_id={axis: lax.rem(mine + step, count)},
                device_id_type=pl.DeviceIdType.MESH,
            )

    loads = [
        pltpu.make_async_copy(source, target, local_sem.at[i])
        for i, (source, target) in enumerate(
            (
                (kv_hbm, kv_ref),
                (mask_hbm, mask_ref),
                (doc_hbm, doc_ref),
                (order_hbm, order_ref),
                (q_hbm, q_ref),
                (g_hbm, g_ref),
            )
        )
    ]
    for load in loads:
        load.start()

    upper = (2 * me) // n
    short = me + upper * (n - 1 - 2 * me)
    spare = n - 1 - 2 * short
    side = 1 - 2 * upper
    far_first = []
    for k in range(n - 1):
        paired = k - spare
        distance = jnp.where(paired < 0, n - 1 - short - k, short - paired // 2)
        turn = jnp.where(paired < 0, 1, 1 - 2 * (paired % 2))
        far_first.append(me + side * turn * distance)

    def remote(source, target, send, recv, axis, peer):
        return pltpu.make_async_remote_copy(
            src_ref=source,
            dst_ref=target,
            send_sem=send,
            recv_sem=recv,
            device_id={axis: peer},
            device_id_type=pl.DeviceIdType.MESH,
        )

    gap = lax.broadcasted_iota(jnp.int32, (chunk, rows), 0) - heads * lax.broadcasted_iota(
        jnp.int32, (chunk, rows), 1
    )
    for c in range(chunks):
        moved = gap + c * chunk
        e_ref[c] = jnp.where((moved >= 0) & (moved < heads), 1.0, 0.0).astype(BF16)
    pick = (
        lax.broadcasted_iota(jnp.int32, (rows, rows * nt), 1)
        - nt * lax.broadcasted_iota(jnp.int32, (rows, rows * nt), 0)
    )
    own_pick = jnp.where(pick == my_head, 1.0, 0.0).astype(BF16)

    loads[0].wait()
    k_own = dot(own_pick, kv_ref[0]).astype(BF16)
    k_all[me] = k_own[skip:]
    v_own = dot(own_pick, kv_ref[1]).astype(BF16)
    v_all[me] = v_own[skip:]
    loads[1].wait()
    counts[me] = mask_ref[...]
    pl.semaphore_wait(barrier, n + nd + nt - 3)

    def kv_copy(i, source, peer):
        held = (k_all, v_all)[i]
        return remote(
            held.at[me], held.at[source], kv_send.at[i, peer], kv_recv.at[i, source], "ctx", peer
        )

    def count_copy(source, peer):
        return remote(
            counts.at[me], counts.at[source], count_send.at[peer], count_recv.at[source], "ctx", peer
        )

    for peer in far_first:
        kv_copy(0, me, peer).start()
    for peer in far_first:
        kv_copy(1, me, peer).start()
    for peer in far_first:
        count_copy(me, peer).start()

    loads[2].wait()
    loads[3].wait()
    own = order_ref[0, me]
    token_row = lax.broadcasted_iota(jnp.int32, (1, rows), 1)
    place_row = own * rows + token_row
    start_row = jnp.zeros((1, rows), jnp.int32)
    bound = jnp.int32(0)
    for j in range(docs):
        bound = bound + doc_ref[0, j]
        start_row = jnp.where(bound <= place_row, bound, start_row)
    key_rows = lax.broadcasted_iota(jnp.int32, (rows, rows), 0)

    def bias_of(target):
        key_places = target * rows + key_rows
        seen = (key_places >= start_row) & (key_places <= place_row)
        return jnp.where(seen, 0.0, HIDDEN).astype(BF16)

    def flipped(block):
        return jnp.transpose(block.astype(F32)).astype(BF16)

    wide_own = jnp.concatenate([k_own, bias_of(own)], axis=1)
    kt_own = flipped(k_own)
    vt_own = flipped(v_own)
    mask_rows = jnp.broadcast_to(mask_ref[...].astype(F32), (8, rows)).astype(BF16)
    turned = lax.broadcasted_iota(jnp.int32, (rows * nt, rows), 0) - nt * lax.broadcasted_iota(
        jnp.int32, (rows * nt, rows), 1
    )
    for h in range(nt):
        spread[h] = jnp.where(turned == h, 1.0, 0.0).astype(BF16)

    def cols(c):
        return pl.ds(c * chunk, chunk)

    def wide_queries(c):
        return jnp.concatenate([q_ref[cols(c), :], e_ref[c]], axis=1)

    loads[4].wait()
    loads[5].wait()
    top, total, drift, kept = [], [], [], []

    def seen_rows(c, behind):
        first = c * CHUNK_TOKENS + behind * rows - (longest - 1)
        low = max(0, first // 16 * 16)
        return low, rows if behind else (c + 1) * CHUNK_TOKENS

    def padded(block, low, high):
        block = block.astype(BF16)
        parts = [block]
        if low:
            parts.insert(0, jnp.zeros((low, chunk), BF16))
        if high < rows:
            parts.append(jnp.zeros((rows - high, chunk), BF16))
        return jnp.concatenate(parts, axis=0) if len(parts) > 1 else block

    def close_own(c, gain, delta):
        low, high = seen_rows(c, 0)
        masked = po_ref[low:high, cols(c)] * gain
        pmo_ref[:, cols(c)] = padded(masked, low, high)
        dso_ref[:, cols(c)] = padded(masked * (dpo_ref[low:high, cols(c)] - delta), low, high)

    for c in range(chunks):
        low, high = seen_rows(c, 0)
        scores = dot_t(wide_own[low:high], wide_queries(c))
        grads = dot_t(v_own[low:high], g_ref[cols(c), :])
        highest = jnp.max(scores, axis=0, keepdims=True)
        raised = jnp.exp2((scores - highest) * steep)
        summed = jnp.sum(raised, axis=0, keepdims=True)
        drifted = jnp.sum(raised * grads, axis=0, keepdims=True)
        top.append(highest)
        total.append(summed)
        drift.append(drifted)
        kept.append(dot_t(mask_rows, e_ref[c])[0:1])
        po_ref[low:high, cols(c)] = raised
        dpo_ref[low:high, cols(c)] = grads
        own_part = dot(vt_own, padded(raised, low, high))
        if c < part_chunks:
            atto_ref[:, cols(c)] = own_part
        else:
            inverse = 1.0 / summed
            close_own(c, kept[c] * inverse, drifted * inverse)
            att_ref[cols(c), :] = jnp.transpose(own_part * inverse).astype(BF16)

    def others():
        return [lax.rem(me + step, n) for step in range(1, n)]

    def filled(block):
        if not skip:
            return block
        return jnp.concatenate([jnp.zeros((skip, width), block.dtype), block], axis=0)

    def grad_copy(i, step):
        return remote(
            staged.at[i, step],
            landed.at[i, step],
            grad_send.at[i, step],
            grad_recv.at[i, step],
            "ctx",
            lax.rem(me + step, n),
        )

    def scatter(i):
        pieces[i, window] = jnp.zeros((tail, width), BF16)
        for step in range(1, n):
            peer = lax.rem(me + step, n)
            chosen = jnp.int32(window)
            for w in range(window):
                chosen = jnp.where(order_ref[0, peer] == targets[w], w, chosen)
            staged[i, step] = pieces[i, chosen]
        for peer in far_first:
            grad_copy(i, lax.rem(peer - me + n, n)).start()

    for peer in others():
        kv_copy(0, peer, peer).wait()
    targets = [own - 1 - w for w in range(window)]
    holders = []
    for w in range(window):
        holder = jnp.int32(0)
        for j in range(n):
            holder = holder + jnp.where(order_ref[0, j] == targets[w], j, 0)
        holders.append(holder)
    keys = [filled(k_all[holders[w]]) for w in range(window)]
    wide = [jnp.concatenate([keys[w], bias_of(targets[w])], axis=1) for w in range(window)]
    gains, inverses, fades = [], [], []
    for c in range(part_chunks):
        queries = wide_queries(c)
        low = [seen_rows(c, w + 1)[0] for w in range(window)]
        scores = [dot_t(wide[w][low[w]:], queries) for w in range(window)]
        highest = top[c]
        for w in range(window):
            highest = jnp.maximum(highest, jnp.max(scores[w], axis=0, keepdims=True))
        fade = jnp.exp2((top[c] - highest) * steep)
        summed = total[c] * fade
        raised = []
        for w in range(window):
            part = jnp.exp2((scores[w] - highest) * steep)
            summed = summed + jnp.sum(part, axis=0, keepdims=True)
            pf_ref[w, low[w]:, cols(c)] = part
            raised.append(part)
        inverse = 1.0 / summed
        gain = kept[c] * inverse
        for w in range(window):
            pmp_ref[w, :, cols(c)] = padded(raised[w] * gain, low[w], rows)
        gains.append(gain)
        inverses.append(inverse)
        fades.append(fade)
    for w in range(window):
        pieces[1, w] = dot(pmp_ref[w], g_ref[:part_rows, :])[skip:].astype(BF16)
    scatter(1)

    for peer in others():
        kv_copy(1, peer, peer).wait()
    values = [filled(v_all[holders[w]]) for w in range(window)]
    deltas = []
    for c in range(part_chunks):
        low = [seen_rows(c, w + 1)[0] for w in range(window)]
        grads = [dot_t(values[w][low[w]:], g_ref[cols(c), :]) for w in range(window)]
        raised = [pf_ref[w, low[w]:, cols(c)] for w in range(window)]
        drifted = drift[c] * fades[c]
        for w in range(window):
            drifted = drifted + jnp.sum(raised[w] * grads[w], axis=0, keepdims=True)
        delta = drifted * inverses[c]
        for w in range(window):
            dsp_ref[w, :, cols(c)] = padded(
                raised[w] * gains[c] * (grads[w] - delta), low[w], rows
            )
        deltas.append(delta)
    for w in range(window):
        pieces[0, w] = (dot(dsp_ref[w], q_ref[:part_rows, :])[skip:] * factor).astype(BF16)
    scatter(0)

    for peer in others():
        count_copy(peer, peer).wait()
    dcounts[my_dp] = jnp.sum(counts[...], axis=0)
    dcount_copies = [
        remote(
            dcounts.at[my_dp],
            dcounts.at[my_dp],
            dcount_send.at[step],
            dcount_recv.at[step],
            "dp",
            lax.rem(my_dp + step, nd),
        )
        for step in range(1, nd)
    ]
    for copy in dcount_copies:
        copy.start()

    def head_copies(buffer, send, recv):
        return [
            remote(
                buffer.at[my_head],
                buffer.at[my_head],
                send.at[step],
                recv.at[step],
                "tensor",
                lax.rem(my_head + step, nt),
            )
            for step in range(1, nt)
        ]

    for c in range(part_chunks):
        close_own(c, gains[c] * fades[c], deltas[c])
    owns[my_head, 0] = (dot(dso_ref[...], q_ref[...]) * factor).astype(BF16)
    owns[my_head, 1] = dot(pmo_ref[...], g_ref[...]).astype(BF16)
    own_copies = head_copies(owns, own_send, own_recv)
    for copy in own_copies:
        copy.start()

    vts = [flipped(values[w]) for w in range(window)]
    for c in range(part_chunks):
        both = atto_ref[:, cols(c)] * fades[c]
        for w in range(window):
            low = seen_rows(c, w + 1)[0]
            both = both + dot(vts[w], padded(pf_ref[w, low:, cols(c)], low, rows))
        att_ref[cols(c), :] = jnp.transpose(both * inverses[c]).astype(BF16)

    def forward(i):
        for step in range(1, n):
            grad_copy(i, step).wait()
        arrived = landed[i, 1].astype(F32)
        for step in range(2, n):
            arrived = arrived + landed[i, step].astype(F32)
        tails[i, my_head] = arrived.astype(BF16)
        copies = head_copies(tails.at[i], tail_send.at[i], tail_recv.at[i])
        for copy in copies:
            copy.start()
        return copies

    tail_v = forward(1)
    for copy in dcount_copies:
        copy.wait()
    counted = jnp.sum(
        jnp.sum(dcounts[...], axis=0).astype(F32), axis=1, keepdims=True
    )
    weight = weight_top / jnp.maximum(counted, 1.0)
    kts = [flipped(keys[w]) for w in range(window)]
    for c in range(chunks):
        back = dot(kt_own, dso_ref[:, cols(c)])
        if c < part_chunks:
            for w in range(window):
                back = back + dot(kts[w], dsp_ref[w, :, cols(c)])
        dq_ref[cols(c), :] = jnp.transpose(back * (weight * factor)).astype(BF16)

    def mixed(blocks):
        result = dot(spread[0], blocks[0])
        for h in range(1, nt):
            result = result + dot(spread[h], blocks[h])
        return result

    for copy in own_copies:
        copy.wait()
    for i in range(2):
        base[i] = mixed([owns[h, i] for h in range(nt)])

    def finish(i, copies):
        for copy in copies:
            copy.wait()
        arrived = mixed([filled(tails[i, h]) for h in range(nt)])
        dkv_ref[i] = ((base[i] + arrived) * weight).astype(BF16)

    tail_k = forward(0)
    finish(1, tail_v)
    finish(0, tail_k)


def write_out(att_ref, dq_ref, dkv_ref, att_hbm, dq_hbm, dkv_hbm, sems):
    pairs = [(dkv_ref.at[i], dkv_hbm.at[i]) for i in range(dkv_ref.shape[0])]
    piece = att_ref.shape[0] // OUT_PIECES
    for i in range(OUT_PIECES):
        span = pl.ds(i * piece, piece)
        pairs.append((att_ref.at[span], att_hbm.at[span]))
        pairs.append((dq_ref.at[span], dq_hbm.at[span]))
    copies = [
        pltpu.make_async_copy(source, target, sems.at[i])
        for i, (source, target) in enumerate(pairs)
    ]
    for copy in copies:
        copy.start()
    for copy in copies:
        copy.wait()


def local(query, key_value, grad_out, doc_lengths, stretch_order, loss_mask):
    _, rows, heads, width = query.shape
    n, nd, nt = lax.axis_size("ctx"), lax.axis_size("dp"), lax.axis_size("tensor")
    length = rows * n
    longest = length * 5 // 32
    window = (longest - 1 + rows - 1) // rows
    tail = rows if window > 1 else -(-(longest - 1) // 16) * 16
    reach = min(rows, longest - 1) if window == 1 else rows
    part_chunks = min(rows // CHUNK_TOKENS, -(-reach // CHUNK_TOKENS))
    docs = doc_lengths.shape[1]
    total = rows * heads
    part = part_chunks * CHUNK_TOKENS * heads
    chunk = CHUNK_TOKENS * heads
    chunks = rows // CHUNK_TOKENS
    weight_top = float(nd * query.shape[0] * length)
    sizes = (n, nd, nt, rows, heads, width, window, tail, docs, longest, part_chunks, weight_top)
    dma = pltpu.SemaphoreType.DMA
    any_spec = pl.BlockSpec(memory_space=pl.ANY)
    vmem_spec = pl.BlockSpec(memory_space=pltpu.VMEM)
    shapes = (
        jax.ShapeDtypeStruct((total, width), BF16),
        jax.ShapeDtypeStruct((total, width), BF16),
        jax.ShapeDtypeStruct((2, rows * nt, width), BF16),
    )
    results = pl.pallas_call(
        functools.partial(kernel, sizes),
        out_shape=shapes,
        in_specs=[pl.BlockSpec(memory_space=pltpu.MemorySpace.HBM)] * 6,
        out_specs=(vmem_spec,) * 3,
        scratch_shapes=[
            pltpu.VMEM((total, width), BF16),
            pltpu.VMEM((2, rows * nt, width), BF16),
            pltpu.VMEM((total, width), BF16),
            pltpu.SMEM((1, docs), jnp.int32),
            pltpu.SMEM((1, n), jnp.int32),
            pltpu.VMEM((1, rows), jnp.int32),
            pltpu.VMEM((n, tail, width), BF16),
            pltpu.VMEM((n, tail, width), BF16),
            pltpu.VMEM((n, 1, rows), jnp.int32),
            pltpu.VMEM((nd, 1, rows), jnp.int32),
            pltpu.VMEM((2, window + 1, tail, width), BF16),
            pltpu.VMEM((2, n, tail, width), BF16),
            pltpu.VMEM((2, n, tail, width), BF16),
            pltpu.VMEM((nt, 2, rows, width), BF16),
            pltpu.VMEM((2, nt, tail, width), BF16),
            pltpu.VMEM((2, rows * nt, width), F32),
            pltpu.VMEM((nt, rows * nt, rows), BF16),
            pltpu.VMEM((chunks, chunk, rows), BF16),
            pltpu.VMEM((rows, total), F32),
            pltpu.VMEM((rows, total), F32),
            pltpu.VMEM((width, part), F32),
            pltpu.VMEM((rows, total), BF16),
            pltpu.VMEM((rows, total), BF16),
            pltpu.VMEM((window, rows, part), F32),
            pltpu.VMEM((window, rows, part), BF16),
            pltpu.VMEM((window, rows, part), BF16),
            dma((6,)),
            dma((2, n)), dma((2, n)),
            dma((n,)), dma((n,)),
            dma((nd,)), dma((nd,)),
            dma((2, n)), dma((2, n)),
            dma((nt,)), dma((nt,)),
            dma((2, nt)), dma((2, nt)),
        ],
        compiler_params=pltpu.CompilerParams(
            collective_id=0, has_side_effects=True, vmem_limit_bytes=KERNEL_VMEM
        ),
        name="packed_attention",
    )(
        *(
            pltpu.with_memory_space_constraint(array, pltpu.MemorySpace.HBM)
            for array in (
                query.reshape(total, width),
                key_value.reshape(2, rows * nt, width),
                grad_out.reshape(total, width),
                doc_lengths,
                stretch_order,
                loss_mask,
            )
        )
    )
    att, dq, dkv = pl.pallas_call(
        write_out,
        out_shape=shapes,
        in_specs=[vmem_spec] * 3,
        out_specs=(any_spec,) * 3,
        scratch_shapes=[dma((2 + 2 * OUT_PIECES,))],
        compiler_params=pltpu.CompilerParams(vmem_limit_bytes=KERNEL_VMEM),
        name="write_out",
    )(*results)
    return (
        att.reshape(query.shape),
        dq.reshape(query.shape),
        dkv.reshape(key_value.shape),
    )


def solution(mesh):
    placed = (
        P("dp", "ctx", "tensor", None),
        P(None, "dp", "ctx", None, None),
        P("dp", "ctx", "tensor", None),
        P("dp", None),
        P("dp", None),
        P("dp", "ctx"),
    )
    return jax.shard_map(
        local,
        mesh=mesh,
        in_specs=placed,
        out_specs=(
            P("dp", "ctx", "tensor", None),
            P("dp", "ctx", "tensor", None),
            P(None, "dp", "ctx", None, None),
        ),
        check_vma=False,
    )
```

```python
import functools
import math

import jax
import jax.numpy as jnp
from jax import lax
from jax.experimental import pallas as pl
from jax.experimental.pallas import tpu as pltpu
from jax.sharding import PartitionSpec as P

HIDDEN = -1e30
CHUNK_TOKENS = 16
KERNEL_VMEM = 32 * 1024 * 1024
OUT_PIECES = 4
F32 = jnp.float32
BF16 = jnp.bfloat16


def dot(left, right):
    return lax.dot_general(left, right, (((1,), (0,)), ((), ())), preferred_element_type=F32)


def dot_t(left, right):
    return lax.dot_general(left, right, (((1,), (1,)), ((), ())), preferred_element_type=F32)


def dot_l(left, right):
    return lax.dot_general(left, right, (((0,), (0,)), ((), ())), preferred_element_type=F32)


def kernel(
    sizes,
    q_hbm, kv_hbm, g_hbm, doc_hbm, order_hbm, mask_hbm,
    att_ref, dq_ref, dkv_ref,
    q_ref, kv_ref, g_ref, doc_ref, order_ref, mask_ref,
    k_all, v_all, counts, dcounts, pieces, staged, landed, owns, tails, base, spread,
    e_ref, po_ref, dpo_ref, atto_ref, pmo_ref, dso_ref, pf_ref, pmp_ref, dsp_ref,
    local_sem, answers, kv_send, kv_recv, count_send, count_recv, dcount_send, dcount_recv,
    grad_send, grad_recv, own_send, own_recv, tail_send, tail_recv,
):
    n, nd, nt, rows, heads, width, window, tail, docs, longest, part_chunks, weight_top = sizes
    me = lax.axis_index("ctx")
    my_dp = lax.axis_index("dp")
    my_head = lax.axis_index("tensor")
    chunk = CHUNK_TOKENS * heads
    chunks = rows // CHUNK_TOKENS
    part_rows = part_chunks * chunk
    skip = rows - tail
    factor = 1.0 / math.sqrt(width)
    steep = factor * math.log2(math.e)

    barrier = pltpu.get_barrier_semaphore()
    for axis, mine, count in (("ctx", me, n), ("tensor", my_head, nt)):
        for step in range(1, count):
            pl.semaphore_signal(
                barrier,
                inc=1,
                device_id={axis: lax.rem(mine + step, count)},
                device_id_type=pl.DeviceIdType.MESH,
            )

    for step in range(1, nd):

        @pl.when(my_dp + step < nd)
        def _greet():
            pl.semaphore_signal(
                barrier,
                inc=1,
                device_id={"dp": lax.rem(my_dp + step, nd)},
                device_id_type=pl.DeviceIdType.MESH,
            )

    loads = [
        pltpu.make_async_copy(source, target, local_sem.at[i])
        for i, (source, target) in enumerate(
            (
                (kv_hbm, kv_ref),
                (mask_hbm, mask_ref),
                (doc_hbm, doc_ref),
                (order_hbm, order_ref),
                (q_hbm, q_ref),
                (g_hbm, g_ref),
            )
        )
    ]
    for load in loads:
        load.start()

    upper = (2 * me) // n
    short = me + upper * (n - 1 - 2 * me)
    spare = n - 1 - 2 * short
    side = 1 - 2 * upper
    far_first = []
    for k in range(n - 1):
        paired = k - spare
        distance = jnp.where(paired < 0, n - 1 - short - k, short - paired // 2)
        turn = jnp.where(paired < 0, 1, 1 - 2 * (paired % 2))
        far_first.append(me + side * turn * distance)

    def remote(source, target, send, recv, axis, peer):
        return pltpu.make_async_remote_copy(
            src_ref=source,
            dst_ref=target,
            send_sem=send,
            recv_sem=recv,
            device_id={axis: peer},
            device_id_type=pl.DeviceIdType.MESH,
        )

    gap = lax.broadcasted_iota(jnp.int32, (chunk, rows), 0) - heads * lax.broadcasted_iota(
        jnp.int32, (chunk, rows), 1
    )
    for c in range(chunks):
        moved = gap + c * chunk
        e_ref[c] = jnp.where((moved >= 0) & (moved < heads), 1.0, 0.0).astype(BF16)
    pick = (
        lax.broadcasted_iota(jnp.int32, (rows, rows * nt), 1)
        - nt * lax.broadcasted_iota(jnp.int32, (rows, rows * nt), 0)
    )
    own_pick = jnp.where(pick == my_head, 1.0, 0.0).astype(BF16)

    loads[0].wait()
    k_own = dot(own_pick, kv_ref[0]).astype(BF16)
    k_all[me] = k_own[skip:]
    v_own = dot(own_pick, kv_ref[1]).astype(BF16)
    v_all[me] = v_own[skip:]
    loads[1].wait()
    counts[me] = mask_ref[...]
    pl.semaphore_wait(barrier, n + nt - 2 + my_dp)

    def kv_copy(i, source, peer):
        held = (k_all, v_all)[i]
        return remote(
            held.at[me], held.at[source], kv_send.at[i, peer], kv_recv.at[i, source], "ctx", peer
        )

    def count_copy(source, peer):
        return remote(
            counts.at[me], counts.at[source], count_send.at[peer], count_recv.at[source], "ctx", peer
        )

    for peer in far_first:
        kv_copy(0, me, peer).start()
    for peer in far_first:
        count_copy(me, peer).start()
    for peer in far_first:
        kv_copy(1, me, peer).start()
    for step in range(1, nd):

        @pl.when(my_dp >= step)
        def _answer():
            pl.semaphore_signal(
                answers,
                inc=1,
                device_id={"dp": lax.rem(my_dp - step + nd, nd)},
                device_id_type=pl.DeviceIdType.MESH,
            )

    loads[2].wait()
    loads[3].wait()
    own = order_ref[0, me]
    token_row = lax.broadcasted_iota(jnp.int32, (1, rows), 1)
    place_row = own * rows + token_row
    start_row = jnp.zeros((1, rows), jnp.int32)
    bound = jnp.int32(0)
    for j in range(docs):
        bound = bound + doc_ref[0, j]
        start_row = jnp.where(bound <= place_row, bound, start_row)
    key_rows = lax.broadcasted_iota(jnp.int32, (rows, rows), 0)

    def bias_of(target):
        key_places = target * rows + key_rows
        seen = (key_places >= start_row) & (key_places <= place_row)
        return jnp.where(seen, 0.0, HIDDEN).astype(BF16)

    def flipped(block):
        return jnp.transpose(block.astype(F32)).astype(BF16)

    wide_own = jnp.concatenate([k_own, bias_of(own)], axis=1)
    kt_own = flipped(k_own)
    vt_own = flipped(v_own)
    mask_rows = jnp.broadcast_to(mask_ref[...].astype(F32), (8, rows)).astype(BF16)
    turned = lax.broadcasted_iota(jnp.int32, (rows * nt, rows), 0) - nt * lax.broadcasted_iota(
        jnp.int32, (rows * nt, rows), 1
    )
    for h in range(nt):
        spread[h] = jnp.where(turned == h, 1.0, 0.0).astype(BF16)

    def cols(c):
        return pl.ds(c * chunk, chunk)

    def wide_queries(c):
        return jnp.concatenate([q_ref[cols(c), :], e_ref[c]], axis=1)

    loads[4].wait()
    loads[5].wait()
    top, total, drift, kept = [], [], [], []

    def seen_rows(c, behind):
        first = c * CHUNK_TOKENS + behind * rows - (longest - 1)
        low = max(0, first // 16 * 16)
        return low, rows if behind else (c + 1) * CHUNK_TOKENS

    def padded(block, low, high):
        block = block.astype(BF16)
        parts = [block]
        if low:
            parts.insert(0, jnp.zeros((low, chunk), BF16))
        if high < rows:
            parts.append(jnp.zeros((rows - high, chunk), BF16))
        return jnp.concatenate(parts, axis=0) if len(parts) > 1 else block

    def close_own(c, gain, delta):
        low, high = seen_rows(c, 0)
        masked = po_ref[low:high, cols(c)] * gain
        pmo_ref[:, cols(c)] = padded(masked, low, high)
        dso_ref[:, cols(c)] = padded(masked * (dpo_ref[low:high, cols(c)] - delta), low, high)

    for c in range(chunks):
        low, high = seen_rows(c, 0)
        scores = dot_t(wide_own[low:high], wide_queries(c))
        grads = dot_t(v_own[low:high], g_ref[cols(c), :])
        highest = jnp.max(scores, axis=0, keepdims=True)
        raised = jnp.exp2((scores - highest) * steep)
        summed = jnp.sum(raised, axis=0, keepdims=True)
        drifted = jnp.sum(raised * grads, axis=0, keepdims=True)
        top.append(highest)
        total.append(summed)
        drift.append(drifted)
        kept.append(dot_t(mask_rows, e_ref[c])[0:1])
        po_ref[low:high, cols(c)] = raised
        dpo_ref[low:high, cols(c)] = grads
        own_part = dot(vt_own, padded(raised, low, high))
        if c < part_chunks:
            atto_ref[:, cols(c)] = own_part
        else:
            inverse = 1.0 / summed
            close_own(c, kept[c] * inverse, drifted * inverse)
            att_ref[cols(c), :] = jnp.transpose(own_part * inverse).astype(BF16)

    def others():
        return [lax.rem(me + step, n) for step in range(1, n)]

    def filled(block):
        if not skip:
            return block
        return jnp.concatenate([jnp.zeros((skip, width), block.dtype), block], axis=0)

    def grad_copy(i, step):
        return remote(
            staged.at[i, step],
            landed.at[i, step],
            grad_send.at[i, step],
            grad_recv.at[i, step],
            "ctx",
            lax.rem(me + step, n),
        )

    def scatter(i):
        pieces[i, window] = jnp.zeros((tail, width), BF16)
        for step in range(1, n):
            peer = lax.rem(me + step, n)
            chosen = jnp.int32(window)
            for w in range(window):
                chosen = jnp.where(order_ref[0, peer] == targets[w], w, chosen)
            staged[i, step] = pieces[i, chosen]
        for peer in far_first:
            grad_copy(i, lax.rem(peer - me + n, n)).start()

    for peer in others():
        kv_copy(0, peer, peer).wait()
    targets = [own - 1 - w for w in range(window)]
    holders = []
    for w in range(window):
        holder = jnp.int32(0)
        for j in range(n):
            holder = holder + jnp.where(order_ref[0, j] == targets[w], j, 0)
        holders.append(holder)
    keys = [filled(k_all[holders[w]]) for w in range(window)]
    wide = [jnp.concatenate([keys[w], bias_of(targets[w])], axis=1) for w in range(window)]
    gains, inverses, fades = [], [], []
    for c in range(part_chunks):
        queries = wide_queries(c)
        low = [seen_rows(c, w + 1)[0] for w in range(window)]
        scores = [dot_t(wide[w][low[w]:], queries) for w in range(window)]
        highest = top[c]
        for w in range(window):
            highest = jnp.maximum(highest, jnp.max(scores[w], axis=0, keepdims=True))
        fade = jnp.exp2((top[c] - highest) * steep)
        summed = total[c] * fade
        raised = []
        for w in range(window):
            part = jnp.exp2((scores[w] - highest) * steep)
            summed = summed + jnp.sum(part, axis=0, keepdims=True)
            pf_ref[w, low[w]:, cols(c)] = part
            raised.append(part)
        inverse = 1.0 / summed
        gain = kept[c] * inverse
        for w in range(window):
            pmp_ref[w, :, cols(c)] = padded(raised[w] * gain, low[w], rows)
        gains.append(gain)
        inverses.append(inverse)
        fades.append(fade)
    for w in range(window):
        pieces[1, w] = dot(pmp_ref[w], g_ref[:part_rows, :])[skip:].astype(BF16)
    scatter(1)

    for peer in others():
        count_copy(peer, peer).wait()
    dcounts[my_dp] = jnp.sum(counts[...], axis=0)
    dcount_copies = [
        remote(
            dcounts.at[my_dp],
            dcounts.at[my_dp],
            dcount_send.at[step],
            dcount_recv.at[step],
            "dp",
            lax.rem(my_dp + step, nd),
        )
        for step in range(1, nd)
    ]

    @pl.when(my_dp < nd - 1)
    def _answered():
        pl.semaphore_wait(answers, nd - 1 - my_dp)

    for copy in dcount_copies:
        copy.start()

    for peer in others():
        kv_copy(1, peer, peer).wait()
    values = [filled(v_all[holders[w]]) for w in range(window)]
    deltas = []
    for c in range(part_chunks):
        low = [seen_rows(c, w + 1)[0] for w in range(window)]
        grads = [dot_t(values[w][low[w]:], g_ref[cols(c), :]) for w in range(window)]
        raised = [pf_ref[w, low[w]:, cols(c)] for w in range(window)]
        drifted = drift[c] * fades[c]
        for w in range(window):
            drifted = drifted + jnp.sum(raised[w] * grads[w], axis=0, keepdims=True)
        delta = drifted * inverses[c]
        for w in range(window):
            dsp_ref[w, :, cols(c)] = padded(
                raised[w] * gains[c] * (grads[w] - delta), low[w], rows
            )
        deltas.append(delta)
    for w in range(window):
        pieces[0, w] = (dot(dsp_ref[w], q_ref[:part_rows, :])[skip:] * factor).astype(BF16)
    scatter(0)

    def head_copies(buffer, send, recv):
        return [
            remote(
                buffer.at[my_head],
                buffer.at[my_head],
                send.at[step],
                recv.at[step],
                "tensor",
                lax.rem(my_head + step, nt),
            )
            for step in range(1, nt)
        ]

    for c in range(part_chunks):
        close_own(c, gains[c] * fades[c], deltas[c])
    owns[my_head, 0] = (dot(dso_ref[...], q_ref[...]) * factor).astype(BF16)
    owns[my_head, 1] = dot(pmo_ref[...], g_ref[...]).astype(BF16)
    own_copies = head_copies(owns, own_send, own_recv)
    for copy in own_copies:
        copy.start()

    vts = [flipped(values[w]) for w in range(window)]
    for c in range(part_chunks):
        both = atto_ref[:, cols(c)] * fades[c]
        for w in range(window):
            low = seen_rows(c, w + 1)[0]
            both = both + dot(vts[w], padded(pf_ref[w, low:, cols(c)], low, rows))
        att_ref[cols(c), :] = jnp.transpose(both * inverses[c]).astype(BF16)

    def forward(i):
        for step in range(1, n):
            grad_copy(i, step).wait()
        arrived = landed[i, 1].astype(F32)
        for step in range(2, n):
            arrived = arrived + landed[i, step].astype(F32)
        tails[i, my_head] = arrived.astype(BF16)
        copies = head_copies(tails.at[i], tail_send.at[i], tail_recv.at[i])
        for copy in copies:
            copy.start()
        return copies

    tail_v = forward(1)
    def mixed(blocks):
        result = dot(spread[0], blocks[0])
        for h in range(1, nt):
            result = result + dot(spread[h], blocks[h])
        return result

    for copy in own_copies:
        copy.wait()
    for i in range(2):
        base[i] = mixed([owns[h, i] for h in range(nt)])

    def finish(i, copies):
        for copy in copies:
            copy.wait()
        arrived = mixed([filled(tails[i, h]) for h in range(nt)])
        dkv_ref[i] = ((base[i] + arrived) * weight).astype(BF16)

    tail_k = forward(0)
    for copy in dcount_copies:
        copy.wait()
    counted = jnp.sum(
        jnp.sum(dcounts[...], axis=0).astype(F32), axis=1, keepdims=True
    )
    weight = weight_top / jnp.maximum(counted, 1.0)
    kts = [flipped(keys[w]) for w in range(window)]
    for c in range(chunks):
        back = dot(kt_own, dso_ref[:, cols(c)])
        if c < part_chunks:
            for w in range(window):
                back = back + dot(kts[w], dsp_ref[w, :, cols(c)])
        dq_ref[cols(c), :] = jnp.transpose(back * (weight * factor)).astype(BF16)

    finish(1, tail_v)
    finish(0, tail_k)


def write_out(att_ref, dq_ref, dkv_ref, att_hbm, dq_hbm, dkv_hbm, sems):
    pairs = [(dkv_ref.at[i], dkv_hbm.at[i]) for i in range(dkv_ref.shape[0])]
    piece = att_ref.shape[0] // OUT_PIECES
    for i in range(OUT_PIECES):
        span = pl.ds(i * piece, piece)
        pairs.append((att_ref.at[span], att_hbm.at[span]))
        pairs.append((dq_ref.at[span], dq_hbm.at[span]))
    copies = [
        pltpu.make_async_copy(source, target, sems.at[i])
        for i, (source, target) in enumerate(pairs)
    ]
    for copy in copies:
        copy.start()
    for copy in copies:
        copy.wait()


def local(query, key_value, grad_out, doc_lengths, stretch_order, loss_mask):
    _, rows, heads, width = query.shape
    n, nd, nt = lax.axis_size("ctx"), lax.axis_size("dp"), lax.axis_size("tensor")
    length = rows * n
    longest = length * 5 // 32
    window = (longest - 1 + rows - 1) // rows
    tail = rows if window > 1 else -(-(longest - 1) // 16) * 16
    reach = min(rows, longest - 1) if window == 1 else rows
    part_chunks = min(rows // CHUNK_TOKENS, -(-reach // CHUNK_TOKENS))
    docs = doc_lengths.shape[1]
    total = rows * heads
    part = part_chunks * CHUNK_TOKENS * heads
    chunk = CHUNK_TOKENS * heads
    chunks = rows // CHUNK_TOKENS
    weight_top = float(nd * query.shape[0] * length)
    sizes = (n, nd, nt, rows, heads, width, window, tail, docs, longest, part_chunks, weight_top)
    dma = pltpu.SemaphoreType.DMA
    any_spec = pl.BlockSpec(memory_space=pl.ANY)
    vmem_spec = pl.BlockSpec(memory_space=pltpu.VMEM)
    shapes = (
        jax.ShapeDtypeStruct((total, width), BF16),
        jax.ShapeDtypeStruct((total, width), BF16),
        jax.ShapeDtypeStruct((2, rows * nt, width), BF16),
    )
    results = pl.pallas_call(
        functools.partial(kernel, sizes),
        out_shape=shapes,
        in_specs=[pl.BlockSpec(memory_space=pltpu.MemorySpace.HBM)] * 6,
        out_specs=(vmem_spec,) * 3,
        scratch_shapes=[
            pltpu.VMEM((total, width), BF16),
            pltpu.VMEM((2, rows * nt, width), BF16),
            pltpu.VMEM((total, width), BF16),
            pltpu.SMEM((1, docs), jnp.int32),
            pltpu.SMEM((1, n), jnp.int32),
            pltpu.VMEM((1, rows), jnp.int32),
            pltpu.VMEM((n, tail, width), BF16),
            pltpu.VMEM((n, tail, width), BF16),
            pltpu.VMEM((n, 1, rows), jnp.int32),
            pltpu.VMEM((nd, 1, rows), jnp.int32),
            pltpu.VMEM((2, window + 1, tail, width), BF16),
            pltpu.VMEM((2, n, tail, width), BF16),
            pltpu.VMEM((2, n, tail, width), BF16),
            pltpu.VMEM((nt, 2, rows, width), BF16),
            pltpu.VMEM((2, nt, tail, width), BF16),
            pltpu.VMEM((2, rows * nt, width), F32),
            pltpu.VMEM((nt, rows * nt, rows), BF16),
            pltpu.VMEM((chunks, chunk, rows), BF16),
            pltpu.VMEM((rows, total), F32),
            pltpu.VMEM((rows, total), F32),
            pltpu.VMEM((width, part), F32),
            pltpu.VMEM((rows, total), BF16),
            pltpu.VMEM((rows, total), BF16),
            pltpu.VMEM((window, rows, part), F32),
            pltpu.VMEM((window, rows, part), BF16),
            pltpu.VMEM((window, rows, part), BF16),
            dma((6,)),
            pltpu.SemaphoreType.REGULAR,
            dma((2, n)), dma((2, n)),
            dma((n,)), dma((n,)),
            dma((nd,)), dma((nd,)),
            dma((2, n)), dma((2, n)),
            dma((nt,)), dma((nt,)),
            dma((2, nt)), dma((2, nt)),
        ],
        compiler_params=pltpu.CompilerParams(
            collective_id=0, has_side_effects=True, vmem_limit_bytes=KERNEL_VMEM
        ),
        name="packed_attention",
    )(
        *(
            pltpu.with_memory_space_constraint(array, pltpu.MemorySpace.HBM)
            for array in (
                query.reshape(total, width),
                key_value.reshape(2, rows * nt, width),
                grad_out.reshape(total, width),
                doc_lengths,
                stretch_order,
                loss_mask,
            )
        )
    )
    att, dq, dkv = pl.pallas_call(
        write_out,
        out_shape=shapes,
        in_specs=[vmem_spec] * 3,
        out_specs=(any_spec,) * 3,
        scratch_shapes=[dma((2 + 2 * OUT_PIECES,))],
        compiler_params=pltpu.CompilerParams(vmem_limit_bytes=KERNEL_VMEM),
        name="write_out",
    )(*results)
    return (
        att.reshape(query.shape),
        dq.reshape(query.shape),
        dkv.reshape(key_value.shape),
    )


def solution(mesh):
    placed = (
        P("dp", "ctx", "tensor", None),
        P(None, "dp", "ctx", None, None),
        P("dp", "ctx", "tensor", None),
        P("dp", None),
        P("dp", None),
        P("dp", "ctx"),
    )
    return jax.shard_map(
        local,
        mesh=mesh,
        in_specs=placed,
        out_specs=(
            P("dp", "ctx", "tensor", None),
            P("dp", "ctx", "tensor", None),
            P(None, "dp", "ctx", None, None),
        ),
        check_vma=False,
    )
```
